128 devices in a mesh: dp: 4 (over y), grid: 32 (over z, x, core).
Axes of the slice: x: 4, y: 4, z: 4, core: 2. Of those that a mesh axis runs over, the one named last changes fastest.
Arguments:
- unembed_feature_matrix: bfloat16 [16, 131072, 512], P('dp', 'grid'), may hold values from -6 to 6
- weight_in: bfloat16 [512, 512], replicated, may hold values from -0.25 to 0.25
- bias_in: float32 [512], replicated, may hold values from -3 to 3
- readout_weight: bfloat16 [512], replicated, may hold values from -0.25 to 0.25
- measured_rainfall: float32 [16, 131072], P('dp', 'grid'), may hold values from -20 to 20
- land_mask: int32 [131072], P('grid'), may hold values 0 or 1
- morton: int32 [32, 4096], P('grid'), may hold values from 0 to 4095, each once within a row
Outputs:
- predicted_rainfall: float32 [16, 131072], P('dp', 'grid')
- patch_prediction_deriv: float32 [16, 131072], P('dp', 'grid')
- penalty_per_example: float32 [16], P('dp')
- inner_coefficient_deriv: float32 [512, 512], P('grid')
- offset_projection_derivs: float32 [2, 512], replicated
The draws below stay inside these ranges and needn't reach their ends.
Inputs may be any that keep to these rules, and one draw needn't show every extreme that they name: `morton`: each row is a permutation of 0 to 4095.
All inputs are finite; a program needn't handle non-finite values. No bound on the sum of `land_mask` on one device may be relied on, other than what follows from the above.
Results may differ from the reference program's by a relative error of at most 0.0029.
Values sent between devices are 32-bit elements; how exact they have to be, the bound alone decides.
No kernel may reach another device: no remote copies, remote signals or barrier semaphores. Data moves between devices by JAX's collectives and lax.ppermute only.
A program may use at most 192 MiB of HBM per device.

```python
import math
import jax
import jax.numpy as jnp
from jax import lax

D = 512
CELLS_DEV = 4096
SAMPLES = 16
TILES = 32
CELLS = 131072
N_GRID = 32


def draw_measured_rainfall(key, part):
    place = jnp.arange(CELLS, dtype=jnp.float32) / CELLS
    noise = jax.random.truncated_normal(key, -6.0, 6.0, (SAMPLES, CELLS), jnp.float32)
    spread = 1.0 + 2.0 * place
    center = 0.8 * jnp.cos(3.14159265 * place)
    return (center[None, :] + spread[None, :] * noise).astype(jnp.float32)


def plant(entries, key, least, top_value):
    dims = entries.shape
    index_at = [jax.random.randint(jax.random.fold_in(key, axis), (), 0, dims[axis]) for axis in range(len(dims))]
    entries = entries.at[tuple(index_at)].set(least)
    longest = dims.index(max(dims))
    index_at[longest] = (index_at[longest] + 1) % dims[longest]
    return entries.at[tuple(index_at)].set(top_value)


def spiked(entries, key, source, target, blocks, factor):
    owner, partner = [(jnp.arange(entries.shape[position]) // (entries.shape[position] // blocks)).reshape([-1 if axis == position else 1 for axis in range(entries.ndim)]) for position in (source, target)]
    chosen = jax.random.permutation(key, blocks)[partner]
    strong = (owner == chosen) | (owner == (partner + blocks // 2) % blocks)
    return jnp.where(strong, factor * entries, entries)


def block_scale(key, shape, pieces, smallest, largest):
    gain, own = 1.0, jax.random.fold_in(key, 6)
    for axis_at, shards_of in pieces:
        heights = jnp.exp(jax.random.uniform(jax.random.fold_in(own, axis_at), (shards_of,), jnp.float32, smallest / len(pieces), largest / len(pieces)))
        gain = gain * jnp.repeat(heights, shape[axis_at] // shards_of).reshape([-1 if axis == axis_at else 1 for axis in range(len(shape))])
    return gain


def gaussian(rng, dims, scale, most, pieces=(), kind=jnp.bfloat16):
    drawn = jax.random.normal(rng, dims, jnp.float32) * scale
    if len(pieces) > 0:
        drawn = block_scale(rng, dims, pieces, -0.22, 0.18) * drawn
    return jnp.clip(drawn, min=-most, max=most).astype(kind)


def noise_with(own_key, dims, scale, bound, cuts, heavy, kind=jnp.bfloat16):
    values = scale * jax.random.normal(own_key, dims, jnp.float32)
    if cuts:
        values = values * block_scale(own_key, dims, cuts, -0.22, 0.18)
    return jnp.clip(spiked(values, jax.random.fold_in(own_key, 3), *heavy), -bound, bound).astype(kind)


def setup_inputs(seed: int = 0) -> dict:
    arg_keys = jax.random.split(jax.random.key(seed), 8)
    unembed_feature_matrix = noise_with(arg_keys[0], (SAMPLES, CELLS, D), 1.0, 6.0, ((0, 4), (1, 32)), (1, 2, 32, 2.75))
    weight_in = gaussian(arg_keys[1], (D, D), D ** -0.5, 0.25)
    bias_in = gaussian(arg_keys[2], (D,), 0.5, 3.0, (), jnp.float32)
    readout_weight = gaussian(arg_keys[3], (D,), D ** -0.5, 0.25)
    measured_rainfall = draw_measured_rainfall(jax.random.fold_in(arg_keys[7], 71), 0)
    land_mask = plant((jax.random.randint(arg_keys[5], (CELLS,), 0, 10) < 3).astype(jnp.int32), jax.random.fold_in(arg_keys[5], 1), 0, 1)
    morton = jax.vmap(lambda own: jax.random.permutation(own, CELLS_DEV))(jax.random.split(arg_keys[6], TILES)).reshape((TILES, CELLS_DEV)).astype(jnp.int32)
    return {"unembed_feature_matrix": unembed_feature_matrix, "weight_in": weight_in, "bias_in": bias_in, "readout_weight": readout_weight, "measured_rainfall": measured_rainfall, "land_mask": land_mask, "morton": morton}


sharpness = 0.5

def smooth_abs(value):
    return jnp.sqrt(1.0 + value * value) - 1.0

def smooth_slope(value):
    return value / jnp.sqrt(1.0 + value * value)

def reference(unembed_feature_matrix, weight_in, bias_in, readout_weight, measured_rainfall, land_mask, morton):
    grad_scale = math.sqrt(D / (SAMPLES * CELLS))
    patch_penalty_factor = 1.0 + land_mask.astype(jnp.float32)
    offsets = (jnp.arange(N_GRID, dtype=jnp.int32) * CELLS_DEV)[:, None]
    zorder_entire = (morton.astype(jnp.int32) + offsets).reshape(-1).astype(jnp.int32)

    def unembed_evaluate(sample_rows):
        preact = jnp.dot(sample_rows, weight_in, preferred_element_type=jnp.float32) + bias_in
        logistic = jax.nn.sigmoid(preact)
        hidden_activation = (preact * logistic).astype(jnp.bfloat16)
        return jnp.dot(hidden_activation, readout_weight, preferred_element_type=jnp.float32)
    predicted_rainfall = lax.map(unembed_evaluate, unembed_feature_matrix)
    prediction_residual = patch_penalty_factor * (predicted_rainfall - measured_rainfall)
    sorted_entries = prediction_residual[:, zorder_entire]
    steepness = jnp.zeros((SAMPLES, CELLS), jnp.float32)
    penalty_per_example = jnp.zeros((SAMPLES,), jnp.float32)
    node_cells = 1
    while node_cells <= CELLS_DEV:
        grouped = sorted_entries.reshape(SAMPLES, CELLS // node_cells, node_cells)
        means = lax.optimization_barrier(jnp.sum(grouped, axis=2)) / node_cells
        penalty_per_example = penalty_per_example + node_cells * lax.optimization_barrier(jnp.sum(smooth_abs(sharpness * means), axis=1))
        steepness = steepness + jnp.repeat(smooth_slope(sharpness * means), node_cells, axis=1)
        node_cells = node_cells * 4
    tile_sums = lax.optimization_barrier(jnp.sum(sorted_entries.reshape(SAMPLES, N_GRID, CELLS_DEV), axis=2))
    groups = []
    group = 4
    while group < N_GRID:
        groups.append(group)
        group = group * 4
    groups.append(N_GRID)
    for group in groups:
        sums = lax.optimization_barrier(jnp.sum(tile_sums.reshape(SAMPLES, N_GRID // group, group), axis=2))
        means = sums / (group * CELLS_DEV)
        penalty_per_example = penalty_per_example + group * CELLS_DEV * lax.optimization_barrier(jnp.sum(smooth_abs(sharpness * means), axis=1))
        steepness = steepness + jnp.repeat(smooth_slope(sharpness * means), group * CELLS_DEV, axis=1)
    penalty_per_example = penalty_per_example / (CELLS * sharpness)
    patch_prediction_deriv = jnp.zeros_like(steepness).at[:, zorder_entire].set(steepness) * patch_penalty_factor

    def reverse_pass(packed):
        sample_rows, grad_row = packed
        preact = jnp.dot(sample_rows, weight_in, preferred_element_type=jnp.float32) + bias_in
        logistic = jax.nn.sigmoid(preact)
        hidden_activation = (preact * logistic).astype(jnp.bfloat16)
        epilogue = (grad_row[:, None] * readout_weight.astype(jnp.float32) * (logistic * (1.0 + preact * (1.0 - logistic)))).astype(jnp.bfloat16)
        weight_term = lax.dot_general(sample_rows, epilogue, (((0,), (0,)), ((), ())), preferred_element_type=jnp.float32)
        bias_term = lax.optimization_barrier(jnp.sum(epilogue.astype(jnp.float32), axis=0))
        out_term = lax.optimization_barrier(jnp.sum(grad_row[:, None] * hidden_activation, axis=0))
        return (weight_term, bias_term, out_term)
    coefficient_summands, offset_summands, final_summands = lax.map(reverse_pass, (unembed_feature_matrix, patch_prediction_deriv))
    inner_coefficient_deriv = grad_scale * lax.optimization_barrier(jnp.sum(coefficient_summands, axis=0))
    offset_projection_derivs = grad_scale * jnp.stack([lax.optimization_barrier(jnp.sum(offset_summands, axis=0)), lax.optimization_barrier(jnp.sum(final_summands, axis=0))])
    return (predicted_rainfall, patch_prediction_deriv, penalty_per_example, inner_coefficient_deriv, offset_projection_derivs)
```

```python
import functools

import jax
import jax.numpy as jnp
from jax import lax
from jax.experimental import pallas as pl
from jax.experimental.pallas import tpu as pltpu
from jax.sharding import Mesh, PartitionSpec as P

F32 = jnp.float32
BF16 = jnp.bfloat16
SHARP = 0.5
LANES = 128
CB = 256
VMEM_LIMIT = 56 << 20


def nt_dot(a, b):
    return lax.dot_general(a, b, (((1,), (1,)), ((), ())), preferred_element_type=F32)


def columns(row, count):
    return jnp.broadcast_to(row, (LANES, count)).T


def smooth_pair(v):
    root = jnp.sqrt(1.0 + v * v)
    return v * v / (1.0 + root), v / root


def load_weights(w_ref, b_ref, r_ref, wt_ref, bcol_ref, rcol_ref):
    width = w_ref.shape[0]
    wt_ref[...] = (0.5 * w_ref[...].astype(F32)).T.astype(BF16)
    bcol_ref[...] = columns(0.5 * b_ref[...], width)
    rcol_ref[...] = columns(r_ref[...].astype(F32), width)


def forward_kernel(
    x_ref, w_ref, b_ref, r_ref, meas_ref, land_ref,
    pred_ref, mm_ref, tot_ref,
    wt_ref, bcol_ref, rcol_ref, z_ref,
):
    step = pl.program_id(0)
    samples = x_ref.shape[0]
    rows = mm_ref.shape[0] // samples

    @pl.when(step == 0)
    def _():
        load_weights(w_ref, b_ref, r_ref, wt_ref, bcol_ref, rcol_ref)

    wt = wt_ref[...]
    width = wt.shape[0]
    bcol = bcol_ref
    rcol = rcol_ref

    def matmul(s):
        z_ref[s] = nt_dot(wt, x_ref[s])

    def elementwise(s):
        for k in range(CB // LANES):
            lane = pl.ds(k * LANES, LANES)
            part = jnp.zeros((8, LANES), F32)
            for u in range(0, width, 64):
                z = z_ref[s, u:u + 64, k * LANES:(k + 1) * LANES] + bcol[u:u + 64, :]
                act = z + z * jnp.tanh(z)
                act = act.astype(BF16).astype(F32) * rcol[u:u + 64, :]
                part = part + jnp.sum(act.reshape(8, 8, LANES), axis=0)
            pred = jnp.sum(part, axis=0, keepdims=True)
            pred_ref[s:s + 1, lane] = pred
            scale = 1.0 + land_ref[:, lane].astype(F32)
            row = s * rows + step * (CB // LANES) + k
            mm_ref[pl.ds(row, 1), :] = scale * (pred - meas_ref[s:s + 1, lane])

    matmul(0)
    for s in range(samples):
        if s + 1 < samples:
            matmul(s + 1)
        elementwise(s)

    @pl.when(step == pl.num_programs(0) - 1)
    def _():
        spot = lax.broadcasted_iota(jnp.int32, (1, LANES), 1)
        total = jnp.zeros((1, LANES), F32)
        for s in range(samples):
            value = jnp.sum(mm_ref[s * rows:(s + 1) * rows, :])
            total = total + jnp.where(spot == s, value, 0.0)
        tot_ref[...] = total


def tree_kernel(mm_ref, morton_ref, slope_ref, loss_ref):
    rows = morton_ref.shape[0]
    samples = mm_ref.shape[0] // rows
    total = samples * rows
    cells = rows * LANES
    place = morton_ref[...]
    high = lax.shift_right_logical(place, 7)
    low = jnp.bitwise_and(place, LANES - 1)

    pieces = []
    for s in range(samples):
        for v in range(0, rows, 8):
            hi_v = high[v:v + 8, :]
            lo_v = low[v:v + 8, :]
            out = jnp.zeros((8, LANES), F32)
            for h in range(rows):
                source = jnp.broadcast_to(mm_ref[s * rows + h:s * rows + h + 1, :], (8, LANES))
                out = jnp.where(hi_v == h, jnp.take_along_axis(source, lo_v, axis=1), out)
            pieces.append(out)
    entries = jnp.concatenate(pieces, axis=0)

    lane = lax.broadcasted_iota(jnp.int32, (total, LANES), 1)
    row = lax.broadcasted_iota(jnp.int32, (total, LANES), 0)

    def pair_lane(value, bit):
        other = jnp.where(
            jnp.bitwise_and(lane, bit) == 0,
            pltpu.roll(value, LANES - bit, 1),
            pltpu.roll(value, bit, 1),
        )
        return value + other

    def pair_row(value, bit):
        other = jnp.where(
            jnp.bitwise_and(row, bit) == 0,
            pltpu.roll(value, total - bit, 0),
            pltpu.roll(value, bit, 0),
        )
        return value + other

    loss, slope = smooth_pair(SHARP * entries)
    sums = entries
    node = 1
    while node < cells:
        for bit in (node, 2 * node):
            if bit < LANES:
                sums = pair_lane(sums, bit)
            else:
                sums = pair_row(sums, bit // LANES)
        node = node * 4
        more_loss, more_slope = smooth_pair((SHARP / node) * sums)
        loss = loss + more_loss
        slope = slope + more_slope

    spot = lax.broadcasted_iota(jnp.int32, (1, LANES), 1)
    loss_row = jnp.zeros((1, LANES), F32)
    for s in range(samples):
        value = jnp.sum(loss[s * rows:(s + 1) * rows, :])
        loss_row = loss_row + jnp.where(spot == s, value, 0.0)
    loss_ref[...] = loss_row

    first = slope.astype(BF16).astype(F32)
    rest = slope - first
    second = rest.astype(BF16).astype(F32)
    third = rest - second
    parts = (first, second, third)
    level = lax.broadcasted_iota(jnp.int32, (rows, LANES), 0)
    spread = lax.broadcasted_iota(jnp.int32, (LANES, LANES), 0)
    placed = jnp.zeros((3 * total, LANES), F32)
    for a in range(0, rows, 2):
        left, right = [], []
        for r in (a, a + 1):
            hit = level == high[r:r + 1, :]
            left.append(jnp.concatenate([
                jnp.where(hit, part[s * rows + r:s * rows + r + 1, :], 0.0)
                for part in parts for s in range(samples)
            ], axis=0))
            right.append(jnp.where(spread == low[r:r + 1, :], 1.0, 0.0))
        placed = placed + nt_dot(
            jnp.concatenate(left, axis=1).astype(BF16),
            jnp.concatenate(right, axis=1).astype(BF16),
        )
    slope_ref[...] = placed[:total] + (placed[total:2 * total] + placed[2 * total:])


def backward_kernel(
    spot_ref, x_ref, w_ref, b_ref, r_ref, slope_ref, land_ref, pairs_ref, loss_ref,
    deriv_ref, keep_ref, send_ref,
    wt_ref, bcol_ref, rcol_ref, coarse_ref, z_ref, e_ref, acc_ref, bias_ref, outp_ref, line_ref,
    *, groups, grad_scale,
):
    step = pl.program_id(0)
    samples = x_ref.shape[0]
    rows = slope_ref.shape[0] // samples
    cells = rows * LANES
    my_z, my_x, my_y, my_c = (spot_ref[n] for n in range(4))
    lane = lax.broadcasted_iota(jnp.int32, (1, LANES), 1)

    @pl.when(step == 0)
    def _():
        load_weights(w_ref, b_ref, r_ref, wt_ref, bcol_ref, rcol_ref)
        acc_ref[...] = jnp.zeros_like(acc_ref)
        bias_ref[...] = jnp.zeros_like(bias_ref)
        outp_ref[...] = jnp.zeros_like(outp_ref)
        pairs = pairs_ref[...]
        index = lax.broadcasted_iota(jnp.int32, pairs.shape, 0)
        mine = my_z * 4 + my_x
        slope = jnp.zeros((1, LANES), F32)
        loss = loss_ref[...]
        for group in groups:
            span = group // 2
            base = mine - lax.rem(mine, span)
            inside = jnp.logical_and(index >= base, index < base + span)
            total = jnp.sum(jnp.where(inside, pairs, 0.0), axis=0, keepdims=True)
            more_loss, more_slope = smooth_pair((SHARP / (group * cells)) * total)
            loss = loss + cells * more_loss
            slope = slope + more_slope
        for s in range(samples):
            value = jnp.sum(jnp.where(lane == s, slope, 0.0))
            coarse_ref[s:s + 1, :] = jnp.broadcast_to(value, (1, LANES))
        own = jnp.logical_and(lane >= my_y * samples, lane < (my_y + 1) * samples)
        line_ref[8:9, :] = jnp.where(own, pltpu.roll(loss, my_y * samples, 1), 0.0)
        line_ref[9:16, :] = jnp.zeros((7, LANES), F32)

    wt = wt_ref[...]
    width = wt.shape[0]

    def matmul(s):
        z_ref[s] = nt_dot(wt, x_ref[s])

    def gradient(s, k):
        row = step * (CB // LANES) + k
        scale = 1.0 + land_ref[pl.ds(row, 1), :].astype(F32)
        local = slope_ref[pl.ds(s * rows + row, 1), :]
        return (local + coarse_ref[s:s + 1, :]) * scale

    def elementwise(s):
        for k in range(CB // LANES):
            span = slice(k * LANES, (k + 1) * LANES)
            grad = gradient(s, k)
            deriv_ref[s:s + 1, span] = grad
            grad8 = jnp.broadcast_to(grad, (8, LANES))
            half8 = 0.5 * grad8
            for u in range(0, width, 64):
                z = z_ref[s, u:u + 64, span] + bcol_ref[u:u + 64, :]
                gate = 1.0 + jnp.tanh(z)
                act = z * gate
                bend = (1.0 + (z + z)) - act
                left = (rcol_ref[u:u + 64, :].reshape(8, 8, LANES) * half8).reshape(64, LANES)
                e = left * (gate * bend)
                e_ref[u:u + 64, s * CB + k * LANES:s * CB + (k + 1) * LANES] = e.astype(BF16)
                bias_ref[u:u + 64, :] += e
                act = act.astype(BF16).astype(F32)
                outp_ref[u:u + 64, :] += (act.reshape(8, 8, LANES) * grad8).reshape(64, LANES)

    matmul(0)
    for s in range(samples):
        if s + 1 < samples:
            matmul(s + 1)
        elementwise(s)
    acc_ref[...] += jnp.dot(
        e_ref[...], x_ref[...].reshape(samples * CB, width), preferred_element_type=F32
    )

    @pl.when(step == pl.num_programs(0) - 1)
    def _():
        acc_ref[...] = (acc_ref[...] * grad_scale).T
        bias = jnp.sum(bias_ref[...].T, axis=0, keepdims=True) * grad_scale
        outp = jnp.sum(outp_ref[...].T, axis=0, keepdims=True) * grad_scale
        for j in range(width // LANES):
            line_ref[j:j + 1, :] = bias[:, j * LANES:(j + 1) * LANES]
            line_ref[4 + j:5 + j, :] = outp[:, j * LANES:(j + 1) * LANES]
        for half, out in ((my_c, keep_ref), (1 - my_c, send_ref)):
            for slot in range(16):
                first = pl.multiple_of(16 * (2 * slot + half), 16)
                for j in range(width // LANES):
                    out[slot * 64 + j * 16:slot * 64 + (j + 1) * 16, :] = acc_ref[
                        pl.ds(first, 16), j * LANES:(j + 1) * LANES
                    ]
            out[1024:1040, :] = line_ref[...]


def whole(shape):
    return pl.BlockSpec(shape, lambda *_: (0,) * len(shape))


def on_device(
    unembed_feature_matrix, weight_in, bias_in, readout_weight, measured_rainfall, land_mask, morton
):
    samples, cells, width = unembed_feature_matrix.shape
    rows = cells // LANES
    tiles = lax.axis_size("z") * lax.axis_size("x") * lax.axis_size("c")
    grad_scale = (width / (samples * lax.axis_size("y") * cells * tiles)) ** 0.5
    steps = cells // CB
    bias_row = bias_in.reshape(1, width)
    readout_row = readout_weight.reshape(1, width)
    land_row = land_mask.reshape(1, cells)
    land_tile = land_mask.reshape(rows, LANES)
    params = pltpu.CompilerParams(
        dimension_semantics=("arbitrary",), vmem_limit_bytes=VMEM_LIMIT
    )
    weight_scratch = [
        pltpu.VMEM((width, width), BF16),
        pltpu.VMEM((width, LANES), F32),
        pltpu.VMEM((width, LANES), F32),
    ]
    x_spec = pl.BlockSpec((samples, CB, width), lambda i: (0, i, 0))
    row_spec = pl.BlockSpec((samples, CB), lambda i: (0, i))

    predicted_rainfall, mismatch, totals = pl.pallas_call(
        forward_kernel,
        grid=(steps,),
        in_specs=[
            x_spec, whole((width, width)), whole((1, width)), whole((1, width)), row_spec,
            pl.BlockSpec((1, CB), lambda i: (0, i)),
        ],
        out_specs=[row_spec, whole((samples * rows, LANES)), whole((1, LANES))],
        out_shape=[
            jax.ShapeDtypeStruct((samples, cells), F32),
            jax.ShapeDtypeStruct((samples * rows, LANES), F32),
            jax.ShapeDtypeStruct((1, LANES), F32),
        ],
        scratch_shapes=weight_scratch + [pltpu.VMEM((samples, width, CB), F32)],
        compiler_params=params,
        name="forward",
    )(unembed_feature_matrix, weight_in, bias_row, readout_row, measured_rainfall, land_row)

    core_pair = totals + lax.ppermute(totals, "c", [(0, 1), (1, 0)])
    pairs = lax.all_to_all(jnp.broadcast_to(core_pair, (16, LANES)), ("z", "x"), 0, 0)

    slope, loss = pl.pallas_call(
        tree_kernel,
        out_shape=[
            jax.ShapeDtypeStruct((samples * rows, LANES), F32),
            jax.ShapeDtypeStruct((1, LANES), F32),
        ],
        name="tree",
    )(mismatch, morton.reshape(rows, LANES))

    spot = jnp.stack([lax.axis_index(name) for name in ("z", "x", "y", "c")]).astype(jnp.int32)
    payload = jax.ShapeDtypeStruct((1040, LANES), F32)
    groups = []
    group = 4
    while group < tiles:
        groups.append(group)
        group = group * 4
    groups.append(tiles)
    patch_prediction_deriv, keep, send = pl.pallas_call(
        functools.partial(backward_kernel, groups=tuple(groups), grad_scale=grad_scale),
        grid_spec=pltpu.PrefetchScalarGridSpec(
            num_scalar_prefetch=1,
            grid=(steps,),
            in_specs=[
                pl.BlockSpec((samples, CB, width), lambda i, _: (0, i, 0)),
                whole((width, width)), whole((1, width)), whole((1, width)),
                whole((samples * rows, LANES)), whole((rows, LANES)),
                whole((16, LANES)), whole((1, LANES)),
            ],
            out_specs=[
                pl.BlockSpec((samples, CB), lambda i, _: (0, i)),
                whole((1040, LANES)), whole((1040, LANES)),
            ],
            scratch_shapes=weight_scratch + [
                pltpu.VMEM((8, LANES), F32),
                pltpu.VMEM((samples, width, CB), F32),
                pltpu.VMEM((width, samples * CB), BF16),
                pltpu.VMEM((width, width), F32),
                pltpu.VMEM((width, LANES), F32),
                pltpu.VMEM((width, LANES), F32),
                pltpu.VMEM((16, LANES), F32),
            ],
        ),
        out_shape=[jax.ShapeDtypeStruct((samples, cells), F32), payload, payload],
        compiler_params=params,
        name="backward",
    )(
        spot, unembed_feature_matrix, weight_in, bias_row, readout_row,
        slope, land_tile, pairs, loss,
    )

    half = keep + lax.ppermute(send, "c", [(0, 1), (1, 0)])
    line = jnp.broadcast_to(half[1024:][None], (16, 16, LANES))
    slots = jnp.concatenate([half[:1024].reshape(16, 64, LANES), line], axis=1)
    own = jnp.sum(lax.all_to_all(slots, ("z", "x"), 0, 0), axis=0)
    for flip in (1, 3):
        own = own + lax.ppermute(own, "y", [(n, n ^ flip) for n in range(4)])
    inner_coefficient_deriv = jnp.concatenate(
        [own[j * 16:(j + 1) * 16] for j in range(width // LANES)], axis=1
    )
    offset_projection_derivs = own[64:72].reshape(2, width)
    penalty_per_example = lax.dynamic_slice_in_dim(
        own[72], lax.axis_index("y") * samples, samples
    ) / (cells * tiles * SHARP)
    return (
        predicted_rainfall,
        patch_prediction_deriv,
        penalty_per_example,
        inner_coefficient_deriv,
        offset_projection_derivs,
    )


def solution(mesh):
    fine = Mesh(mesh.devices.reshape(4, 4, 4, 2), ("y", "z", "x", "c"))
    tile = ("z", "x", "c")
    return jax.shard_map(
        on_device,
        mesh=fine,
        in_specs=(
            P("y", tile, None), P(), P(), P(), P("y", tile), P(tile), P(tile, None),
        ),
        out_specs=(P("y", tile), P("y", tile), P("y"), P(tile, None), P()),
        check_vma=False,
    )
```

```python
import functools

import jax
import jax.numpy as jnp
from jax import lax
from jax.experimental import pallas as pl
from jax.experimental.pallas import tpu as pltpu
from jax.sharding import Mesh, PartitionSpec as P

F32 = jnp.float32
BF16 = jnp.bfloat16
SHARP = 0.5
LANES = 128
CF = 512
CB = 256
UF = 16
UR = 32
VMEM_LIMIT = 56 << 20
KEPT = 1


def nt_dot(a, b):
    return lax.dot_general(a, b, (((1,), (1,)), ((), ())), preferred_element_type=F32)


def columns(row, count):
    return jnp.broadcast_to(row, (LANES, count)).T


def smooth_pair(v):
    root = jnp.sqrt(1.0 + v * v)
    return v * v / (1.0 + root), v / root


def forward_kernel(
    x_ref, w_ref, b_ref, r_ref, meas_ref, land_ref,
    pred_ref, mm_ref, tot_ref, h_ref, act_ref,
    wt_ref, bcol_ref, r8_ref, *rest,
):
    z_refs, spare_refs = rest[:4], rest[4:]
    step = pl.program_id(0)
    samples = x_ref.shape[0]
    rows = mm_ref.shape[0] // samples
    width = w_ref.shape[0]

    @pl.when(step == 0)
    def _():
        wt_ref[...] = (0.5 * w_ref[...].astype(F32)).T.astype(BF16)
        bcol_ref[...] = columns(0.5 * b_ref[...], width)
        r8_ref[...] = jnp.broadcast_to(r_ref[...], r8_ref.shape).astype(BF16)

    wt = wt_ref[...]
    readout8 = r8_ref[...]

    def matmul(s):
        z_refs[s][...] = nt_dot(wt, x_ref[s])

    def elementwise(s):
        for u in range(0, width, UF):
            bias = bcol_ref[u:u + UF, :]
            hs, acts = [], []
            for k in range(CF // LANES):
                z = z_refs[s][u:u + UF, k * LANES:(k + 1) * LANES] + bias
                t = jnp.tanh(z)
                gate = 1.0 + t
                act = z * gate
                if s < KEPT:
                    hs.append(gate + act * (1.0 - t))
                acts.append(act.astype(BF16))
            acts = jnp.concatenate(acts, axis=1)
            spare_refs[s][u:u + UF, :] = acts
            if s < KEPT:
                h_ref[s, u:u + UF, :] = jnp.concatenate(hs, axis=1)
                act_ref[s, u:u + UF, :] = acts

    def readout(s, block):
        preds = jnp.dot(readout8, spare_refs[s][...], preferred_element_type=F32)
        for k in range(CF // LANES):
            lane = pl.ds(pl.multiple_of(block * CF + k * LANES, LANES), LANES)
            pred = preds[0:1, k * LANES:(k + 1) * LANES]
            pred_ref[s:s + 1, lane] = pred
            scale = 1.0 + land_ref[:, lane].astype(F32)
            row = s * rows + block * (CF // LANES) + k
            mm_ref[pl.ds(row, 1), :] = scale * (pred - meas_ref[s:s + 1, lane])

    before = jnp.maximum(step - 1, 0)
    readout(0, before)
    readout(1, before)
    elementwise(2)
    matmul(0)
    elementwise(3)
    matmul(1)
    readout(2, before)
    elementwise(0)
    matmul(2)
    readout(3, before)
    elementwise(1)
    matmul(3)

    @pl.when(step == pl.num_programs(0) - 1)
    def _():
        elementwise(2)
        elementwise(3)
        for s in range(samples):
            readout(s, step)
        spot = lax.broadcasted_iota(jnp.int32, tot_ref.shape, 1)
        total = jnp.zeros(tot_ref.shape, F32)
        for s in range(samples):
            value = jnp.sum(mm_ref[s * rows:(s + 1) * rows, :])
            total = total + jnp.where(spot == s, value, 0.0)
        tot_ref[...] = total


def tree_kernel(mm_ref, morton_ref, slope_ref, loss_ref):
    rows = morton_ref.shape[0]
    samples = mm_ref.shape[0] // rows
    total = samples * rows
    cells = rows * LANES
    place = morton_ref[...]
    high = lax.shift_right_logical(place, 7)
    low = jnp.bitwise_and(place, LANES - 1)

    pieces = []
    for s in range(samples):
        for v in range(0, rows, 8):
            hi_v = high[v:v + 8, :]
            lo_v = low[v:v + 8, :]
            out = jnp.zeros((8, LANES), F32)
            for h in range(rows):
                source = jnp.broadcast_to(mm_ref[s * rows + h:s * rows + h + 1, :], (8, LANES))
                out = jnp.where(hi_v == h, jnp.take_along_axis(source, lo_v, axis=1), out)
            pieces.append(out)
    entries = jnp.concatenate(pieces, axis=0)

    lane = lax.broadcasted_iota(jnp.int32, (total, LANES), 1)
    row = lax.broadcasted_iota(jnp.int32, (total, LANES), 0)

    def pair_lane(value, bit):
        other = jnp.where(
            jnp.bitwise_and(lane, bit) == 0,
            pltpu.roll(value, LANES - bit, 1),
            pltpu.roll(value, bit, 1),
        )
        return value + other

    def pair_row(value, bit):
        other = jnp.where(
            jnp.bitwise_and(row, bit) == 0,
            pltpu.roll(value, total - bit, 0),
            pltpu.roll(value, bit, 0),
        )
        return value + other

    loss, slope = smooth_pair(SHARP * entries)
    sums = entries
    node = 1
    while node < cells:
        for bit in (node, 2 * node):
            if bit < LANES:
                sums = pair_lane(sums, bit)
            else:
                sums = pair_row(sums, bit // LANES)
        node = node * 4
        more_loss, more_slope = smooth_pair((SHARP / node) * sums)
        loss = loss + more_loss
        slope = slope + more_slope

    spot = lax.broadcasted_iota(jnp.int32, (1, LANES), 1)
    loss_row = jnp.zeros((1, LANES), F32)
    for s in range(samples):
        value = jnp.sum(loss[s * rows:(s + 1) * rows, :])
        loss_row = loss_row + jnp.where(spot == s, value, 0.0)
    loss_ref[...] = loss_row

    first = slope.astype(BF16).astype(F32)
    rest = slope - first
    second = rest.astype(BF16).astype(F32)
    third = rest - second
    parts = (first, second, third)
    level = lax.broadcasted_iota(jnp.int32, (rows, LANES), 0)
    spread = lax.broadcasted_iota(jnp.int32, (LANES, LANES), 0)
    placed = jnp.zeros((3 * total, LANES), F32)
    for a in range(0, rows, 2):
        left, right = [], []
        for r in (a, a + 1):
            hit = level == high[r:r + 1, :]
            left.append(jnp.concatenate([
                jnp.where(hit, part[s * rows + r:s * rows + r + 1, :], 0.0)
                for part in parts for s in range(samples)
            ], axis=0))
            right.append(jnp.where(spread == low[r:r + 1, :], 1.0, 0.0))
        placed = placed + nt_dot(
            jnp.concatenate(left, axis=1).astype(BF16),
            jnp.concatenate(right, axis=1).astype(BF16),
        )
    slope_ref[...] = placed[:total] + (placed[total:2 * total] + placed[2 * total:])


def backward_kernel(
    x_ref, late_ref, next_ref, tail_ref, w_ref, b_ref, r_ref, slope_ref, land_ref, pairs_ref, loss_ref, h_ref, act_ref,
    deriv_ref, keep_ref, send_ref,
    wt_ref, bcol_ref, rcol_ref, coarse_ref, z1_ref, z2_ref, z3_ref, e_ref, f_ref, acc_ref, bias_ref, outp_ref, line_ref,
    *, groups, grad_scale,
):
    step = pl.program_id(0)
    samples = deriv_ref.shape[0]
    rows = slope_ref.shape[0] // samples
    cells = rows * LANES
    width = x_ref.shape[2]
    my_z, my_x, my_y, my_c = (lax.axis_index(name) for name in ("z", "x", "y", "c"))
    lane = lax.broadcasted_iota(jnp.int32, (1, LANES), 1)

    z_refs = (z1_ref, z2_ref, z3_ref)

    def matmul(s, block):
        z_refs[s - KEPT][...] = nt_dot(wt_ref[...], block)

    @pl.when(step == 0)
    def _():
        wt_ref[...] = (0.5 * w_ref[...].astype(F32)).T.astype(BF16)
        bcol_ref[...] = columns(0.5 * b_ref[...], width)
        rcol_ref[...] = columns(0.5 * r_ref[...], width)
        acc_ref[...] = jnp.zeros_like(acc_ref)
        bias_ref[...] = jnp.zeros_like(bias_ref)
        outp_ref[...] = jnp.zeros_like(outp_ref)
        e_ref[...] = jnp.zeros_like(e_ref)
        matmul(1, late_ref[1])
        matmul(2, x_ref[0])
        matmul(3, x_ref[1])
        pairs = pairs_ref[...]
        index = lax.broadcasted_iota(jnp.int32, pairs.shape, 0)
        mine = my_z * 4 + my_x
        slope = jnp.zeros((1, LANES), F32)
        loss = loss_ref[...]
        for group in groups:
            span = group // 2
            base = mine - lax.rem(mine, span)
            inside = jnp.logical_and(index >= base, index < base + span)
            total = jnp.sum(jnp.where(inside, pairs, 0.0), axis=0, keepdims=True)
            more_loss, more_slope = smooth_pair((SHARP / (group * cells)) * total)
            loss = loss + cells * more_loss
            slope = slope + more_slope
        for s in range(samples):
            value = jnp.sum(jnp.where(lane == s, slope, 0.0))
            coarse_ref[s:s + 1, :] = jnp.broadcast_to(value, (1, LANES))
        own = jnp.logical_and(lane >= my_y * samples, lane < (my_y + 1) * samples)
        line_ref[8:9, :] = jnp.where(own, pltpu.roll(loss, my_y * samples, 1), 0.0)
        line_ref[9:16, :] = jnp.zeros((7, LANES), F32)

    quarter = width // 4

    def gradients(s):
        grads = []
        for k in range(CB // LANES):
            row = step * (CB // LANES) + k
            scale = 1.0 + land_ref[pl.ds(row, 1), :].astype(F32)
            local = slope_ref[pl.ds(s * rows + row, 1), :]
            grad = (local + coarse_ref[s:s + 1, :]) * scale
            deriv_ref[s:s + 1, k * LANES:(k + 1) * LANES] = grad
            grads.append(jnp.broadcast_to(grad, (UR, LANES)))
        return grads

    def elementwise(s, out_ref, place, grads, *quarters):
        for u in (u for q in quarters for u in range(q * quarter, (q + 1) * quarter, UR)):
            readout = rcol_ref[u:u + UR, :]
            es = []
            bias = outp = None
            for k in range(CB // LANES):
                span = slice(k * LANES, (k + 1) * LANES)
                if s < KEPT:
                    h = h_ref[s, u:u + UR, span]
                    act = act_ref[s, u:u + UR, span]
                else:
                    z = z_refs[s - KEPT][u:u + UR, span] + bcol_ref[u:u + UR, :]
                    t = jnp.tanh(z)
                    gate = 1.0 + t
                    act = z * gate
                    h = gate + act * (1.0 - t)
                    act = act.astype(BF16)
                e = (readout * grads[k]) * h
                a = act.astype(F32) * grads[k]
                es.append(e.astype(BF16))
                bias = e if bias is None else bias + e
                outp = a if outp is None else outp + a
            out_ref[u:u + UR, place * CB:(place + 1) * CB] = jnp.concatenate(es, axis=1)
            bias_ref[u:u + UR, :] += bias
            outp_ref[u:u + UR, :] += outp

    def accumulate(e, x, half):
        span = slice(half * (width // 2), (half + 1) * (width // 2))
        acc_ref[:, span] += jnp.dot(
            e[...], x[:, :, span].reshape(2 * CB, width // 2), preferred_element_type=F32
        )

    grads = [gradients(s) for s in range(samples)]
    first = functools.partial(elementwise, 2, f_ref, 0, grads[2])
    second = functools.partial(elementwise, 3, f_ref, 1, grads[3])
    third = functools.partial(elementwise, 0, e_ref, 0, grads[0])
    fourth = functools.partial(elementwise, 1, e_ref, 1, grads[1])
    first(0)
    accumulate(e_ref, late_ref, 0)
    first(1, 2)
    accumulate(e_ref, late_ref, 1)
    first(3)
    second(0)
    matmul(2, next_ref[2])
    second(1, 2, 3)
    accumulate(f_ref, x_ref, 0)
    fourth(0, 1)
    matmul(3, next_ref[3])
    fourth(2, 3)
    accumulate(f_ref, x_ref, 1)
    matmul(1, next_ref[1])
    third(0, 1, 2, 3)

    @pl.when(step == pl.num_programs(0) - 1)
    def _():
        accumulate(e_ref, tail_ref, 0)
        accumulate(e_ref, tail_ref, 1)
        acc_ref[...] = (acc_ref[...] * grad_scale).T
        bias = jnp.sum(bias_ref[...].T, axis=0, keepdims=True) * grad_scale
        outp = jnp.sum(outp_ref[...].T, axis=0, keepdims=True) * grad_scale
        for j in range(width // LANES):
            line_ref[j:j + 1, :] = bias[:, j * LANES:(j + 1) * LANES]
            line_ref[4 + j:5 + j, :] = outp[:, j * LANES:(j + 1) * LANES]
        for half, out in ((my_c, keep_ref), (1 - my_c, send_ref)):
            for slot in range(16):
                first = pl.multiple_of(16 * (2 * slot + half), 16)
                for j in range(width // LANES):
                    out[slot * 64 + j * 16:slot * 64 + (j + 1) * 16, :] = acc_ref[
                        pl.ds(first, 16), j * LANES:(j + 1) * LANES
                    ]
            out[1024:1040, :] = line_ref[...]


def whole(shape):
    return pl.BlockSpec(shape, lambda *_: (0,) * len(shape))


def on_device(
    unembed_feature_matrix, weight_in, bias_in, readout_weight, measured_rainfall, land_mask, morton
):
    samples, cells, width = unembed_feature_matrix.shape
    rows = cells // LANES
    tiles = lax.axis_size("z") * lax.axis_size("x") * lax.axis_size("c")
    grad_scale = (width / (samples * lax.axis_size("y") * cells * tiles)) ** 0.5
    steps = cells // CB
    bias_row = bias_in.reshape(1, width)
    readout_row = readout_weight.astype(F32).reshape(1, width)
    land_row = land_mask.reshape(1, cells)
    land_tile = land_mask.reshape(rows, LANES)
    params = pltpu.CompilerParams(
        dimension_semantics=("arbitrary",),
        vmem_limit_bytes=VMEM_LIMIT,
    )
    x_spec = pl.BlockSpec((samples, CF, width), lambda i: (0, i, 0))
    row_spec = pl.BlockSpec((samples, CF), lambda i: (0, i))

    kept_spec = pl.BlockSpec((KEPT, width, CF), lambda i: (i, 0, 0))
    predicted_rainfall, mismatch, totals, bend, activated = pl.pallas_call(
        forward_kernel,
        grid=(cells // CF,),
        in_specs=[
            x_spec, whole((width, width)), whole((1, width)), whole((1, width)),
            whole((samples, cells)), whole((1, cells)),
        ],
        out_specs=[
            whole((samples, cells)), whole((samples * rows, LANES)), whole((16, LANES)),
            kept_spec, kept_spec,
        ],
        out_shape=[
            jax.ShapeDtypeStruct((samples, cells), F32),
            jax.ShapeDtypeStruct((samples * rows, LANES), F32),
            jax.ShapeDtypeStruct((16, LANES), F32),
            jax.ShapeDtypeStruct((cells // CF * KEPT, width, CF), F32),
            jax.ShapeDtypeStruct((cells // CF * KEPT, width, CF), BF16),
        ],
        scratch_shapes=[
            pltpu.VMEM((width, width), BF16),
            pltpu.VMEM((width, LANES), F32),
            pltpu.VMEM((16, width), BF16),
        ] + [pltpu.VMEM((width, CF), F32)] * 4 + [pltpu.VMEM((width, CF), BF16)] * 4,
        compiler_params=params,
        name="forward",
    )(
        unembed_feature_matrix, weight_in, bias_row, readout_row, measured_rainfall, land_row,
    )

    kept_spec = pl.BlockSpec((KEPT, width, CB), lambda i: (i // 2, 0, i % 2))
    core_pair = totals + lax.ppermute(totals, "c", [(0, 1), (1, 0)])
    pairs = lax.all_to_all(core_pair, ("z", "x"), 0, 0)

    slope, loss = pl.pallas_call(
        tree_kernel,
        out_shape=[
            jax.ShapeDtypeStruct((samples * rows, LANES), F32),
            jax.ShapeDtypeStruct((1, LANES), F32),
        ],
        name="tree",
    )(mismatch, morton.reshape(rows, LANES))

    payload = jax.ShapeDtypeStruct((1040, LANES), F32)
    groups = []
    group = 4
    while group < tiles:
        groups.append(group)
        group = group * 4
    groups.append(tiles)
    patch_prediction_deriv, keep, send = pl.pallas_call(
        functools.partial(backward_kernel, groups=tuple(groups), grad_scale=grad_scale),
        grid_spec=pltpu.PrefetchScalarGridSpec(
            num_scalar_prefetch=0,
            grid=(steps,),
            in_specs=[
                pl.BlockSpec((2, CB, width), lambda i: (1, i, 0)),
                pl.BlockSpec((2, CB, width), lambda i: (0, jnp.maximum(i - 1, 0), 0)),
                pl.BlockSpec((4, CB, width), lambda i: (0, jnp.minimum(i + 1, steps - 1), 0)),
                pl.BlockSpec((2, CB, width), lambda i: (0, steps - 1, 0)),
                whole((width, width)), whole((1, width)), whole((1, width)),
                whole((samples * rows, LANES)), whole((rows, LANES)),
                whole((16, LANES)), whole((1, LANES)), kept_spec, kept_spec,
            ],
            out_specs=[
                pl.BlockSpec((samples, CB), lambda i: (0, i)),
                whole((1040, LANES)), whole((1040, LANES)),
            ],
            scratch_shapes=[
                pltpu.VMEM((width, width), BF16),
                pltpu.VMEM((width, LANES), F32),
                pltpu.VMEM((width, LANES), F32),
                pltpu.VMEM((8, LANES), F32),
                pltpu.VMEM((width, CB), F32),
                pltpu.VMEM((width, CB), F32),
                pltpu.VMEM((width, CB), F32),
                pltpu.VMEM((width, 2 * CB), BF16),
                pltpu.VMEM((width, 2 * CB), BF16),
                pltpu.VMEM((width, width), F32),
                pltpu.VMEM((width, LANES), F32),
                pltpu.VMEM((width, LANES), F32),
                pltpu.VMEM((16, LANES), F32),
            ],
        ),
        out_shape=[jax.ShapeDtypeStruct((samples, cells), F32), payload, payload],
        compiler_params=params,
        name="backward",
    )(
        *(unembed_feature_matrix,) * 4, weight_in, bias_row, readout_row,
        slope, land_tile, pairs, loss, bend, activated,
    )

    half = keep + lax.ppermute(send, "c", [(0, 1), (1, 0)])
    line = jnp.broadcast_to(half[1024:][None], (16, 16, LANES))
    slots = jnp.concatenate([half[:1024].reshape(16, 64, LANES), line], axis=1)
    own = jnp.sum(lax.all_to_all(slots, ("z", "x"), 0, 0), axis=0)
    for flip in (1, 3):
        own = own + lax.ppermute(own, "y", [(n, n ^ flip) for n in range(4)])
    inner_coefficient_deriv = jnp.concatenate(
        [own[j * 16:(j + 1) * 16] for j in range(width // LANES)], axis=1
    )
    offset_projection_derivs = own[64:72].reshape(2, width)
    penalty_per_example = lax.dynamic_slice_in_dim(
        own[72], lax.axis_index("y") * samples, samples
    ) / (cells * tiles * SHARP)
    return (
        predicted_rainfall,
        patch_prediction_deriv,
        penalty_per_example,
        inner_coefficient_deriv,
        offset_projection_derivs,
    )


def solution(mesh):
    fine = Mesh(mesh.devices.reshape(4, 4, 4, 2), ("y", "z", "x", "c"))
    tile = ("z", "x", "c")
    return jax.shard_map(
        on_device,
        mesh=fine,
        in_specs=(
            P("y", tile, None), P(), P(), P(), P("y", tile), P(tile), P(tile, None),
        ),
        out_specs=(P("y", tile), P("y", tile), P("y"), P(tile, None), P()),
        check_vma=False,
    )
```

```python
import functools

import jax
import jax.numpy as jnp
from jax import lax
from jax.experimental import pallas as pl
from jax.experimental.pallas import tpu as pltpu
from jax.sharding import Mesh, PartitionSpec as P

F32 = jnp.float32
BF16 = jnp.bfloat16
SHARP = 0.5
LANES = 128
CF = 512
CB = 256
UF = 16
UR = 32
VMEM_LIMIT = 56 << 20
KEPT = 1


def nt_dot(a, b):
    return lax.dot_general(a, b, (((1,), (1,)), ((), ())), preferred_element_type=F32)


def columns(row, count):
    return jnp.broadcast_to(row, (LANES, count)).T


def smooth_pair(v):
    root = jnp.sqrt(1.0 + v * v)
    return v * v / (1.0 + root), v / root


def forward_kernel(
    x_ref, w_ref, b_ref, r_ref, meas_ref, land_ref,
    pred_ref, mm_ref, tot_ref, h_ref, act_ref,
    wt_ref, bcol_ref, r8_ref, *rest,
):
    z_refs, spare_refs = rest[:4], rest[4:]
    step = pl.program_id(0)
    samples = x_ref.shape[0]
    rows = mm_ref.shape[0] // samples
    width = w_ref.shape[0]

    @pl.when(step == 0)
    def _():
        wt_ref[...] = (0.5 * w_ref[...].astype(F32)).T.astype(BF16)
        bcol_ref[...] = columns(0.5 * b_ref[...], width)
        r8_ref[...] = jnp.broadcast_to(r_ref[...].astype(F32).reshape(1, width), r8_ref.shape).astype(BF16)

    wt = wt_ref[...]
    readout8 = r8_ref[...]

    def matmul(s):
        z_refs[s][...] = nt_dot(wt, x_ref[s])

    def elementwise(s):
        for u in range(0, width, UF):
            bias = bcol_ref[u:u + UF, :]
            hs, acts = [], []
            for k in range(CF // LANES):
                z = z_refs[s][u:u + UF, k * LANES:(k + 1) * LANES] + bias
                t = jnp.tanh(z)
                gate = 1.0 + t
                act = z * gate
                if s < KEPT:
                    hs.append(gate + act * (1.0 - t))
                acts.append(act.astype(BF16))
            acts = jnp.concatenate(acts, axis=1)
            spare_refs[s][u:u + UF, :] = acts
            if s < KEPT:
                h_ref[s, u:u + UF, :] = jnp.concatenate(hs, axis=1)
                act_ref[s, u:u + UF, :] = acts

    def readout(s, block):
        preds = jnp.dot(readout8, spare_refs[s][...], preferred_element_type=F32)
        for k in range(CF // LANES):
            lane = pl.ds(pl.multiple_of(block * CF + k * LANES, LANES), LANES)
            pred = preds[0:1, k * LANES:(k + 1) * LANES]
            pred_ref[s:s + 1, lane] = pred
            scale = 1.0 + land_ref[:, lane].astype(F32)
            row = s * rows + block * (CF // LANES) + k
            mm_ref[pl.ds(row, 1), :] = scale * (pred - meas_ref[s:s + 1, lane])

    before = jnp.maximum(step - 1, 0)
    readout(0, before)
    readout(1, before)
    elementwise(2)
    matmul(0)
    elementwise(3)
    matmul(1)
    readout(2, before)
    elementwise(0)
    matmul(2)
    readout(3, before)
    elementwise(1)
    matmul(3)

    @pl.when(step == pl.num_programs(0) - 1)
    def _():
        elementwise(2)
        elementwise(3)
        for s in range(samples):
            readout(s, step)
        spot = lax.broadcasted_iota(jnp.int32, tot_ref.shape, 1)
        total = jnp.zeros(tot_ref.shape, F32)
        for s in range(samples):
            value = jnp.sum(mm_ref[s * rows:(s + 1) * rows, :])
            total = total + jnp.where(spot == s, value, 0.0)
        tot_ref[...] = total


def tree_kernel(mm_ref, morton_ref, slope_ref, loss_ref):
    rows = morton_ref.shape[0]
    samples = mm_ref.shape[0] // rows
    total = samples * rows
    cells = rows * LANES
    place = morton_ref[...]
    high = lax.shift_right_logical(place, 7)
    low = jnp.bitwise_and(place, LANES - 1)

    pieces = []
    for s in range(samples):
        for v in range(0, rows, 8):
            hi_v = high[v:v + 8, :]
            lo_v = low[v:v + 8, :]
            out = jnp.zeros((8, LANES), F32)
            for h in range(rows):
                source = jnp.broadcast_to(mm_ref[s * rows + h:s * rows + h + 1, :], (8, LANES))
                out = jnp.where(hi_v == h, jnp.take_along_axis(source, lo_v, axis=1), out)
            pieces.append(out)
    entries = jnp.concatenate(pieces, axis=0)

    lane = lax.broadcasted_iota(jnp.int32, (total, LANES), 1)
    row = lax.broadcasted_iota(jnp.int32, (total, LANES), 0)

    def pair_lane(value, bit):
        other = jnp.where(
            jnp.bitwise_and(lane, bit) == 0,
            pltpu.roll(value, LANES - bit, 1),
            pltpu.roll(value, bit, 1),
        )
        return value + other

    def pair_row(value, bit):
        other = jnp.where(
            jnp.bitwise_and(row, bit) == 0,
            pltpu.roll(value, total - bit, 0),
            pltpu.roll(value, bit, 0),
        )
        return value + other

    loss, slope = smooth_pair(SHARP * entries)
    sums = entries
    node = 1
    while node < cells:
        for bit in (node, 2 * node):
            if bit < LANES:
                sums = pair_lane(sums, bit)
            else:
                sums = pair_row(sums, bit // LANES)
        node = node * 4
        more_loss, more_slope = smooth_pair((SHARP / node) * sums)
        loss = loss + more_loss
        slope = slope + more_slope

    spot = lax.broadcasted_iota(jnp.int32, (1, LANES), 1)
    loss_row = jnp.zeros((1, LANES), F32)
    for s in range(samples):
        value = jnp.sum(loss[s * rows:(s + 1) * rows, :])
        loss_row = loss_row + jnp.where(spot == s, value, 0.0)
    loss_ref[...] = loss_row

    first = slope.astype(BF16).astype(F32)
    rest = slope - first
    second = rest.astype(BF16).astype(F32)
    third = rest - second
    parts = (first, second, third)
    level = lax.broadcasted_iota(jnp.int32, (rows, LANES), 0)
    spread = lax.broadcasted_iota(jnp.int32, (LANES, LANES), 0)
    placed = jnp.zeros((3 * total, LANES), F32)
    for a in range(0, rows, 2):
        left, right = [], []
        for r in (a, a + 1):
            hit = level == high[r:r + 1, :]
            left.append(jnp.concatenate([
                jnp.where(hit, part[s * rows + r:s * rows + r + 1, :], 0.0)
                for part in parts for s in range(samples)
            ], axis=0))
            right.append(jnp.where(spread == low[r:r + 1, :], 1.0, 0.0))
        placed = placed + nt_dot(
            jnp.concatenate(left, axis=1).astype(BF16),
            jnp.concatenate(right, axis=1).astype(BF16),
        )
    slope_ref[...] = placed[:total] + (placed[total:2 * total] + placed[2 * total:])


def backward_kernel(
    x_ref, late_ref, next_ref, tail_ref, w_ref, b_ref, r_ref, slope_ref, land_ref, same_ref, other_ref, loss_ref, h_ref, act_ref,
    deriv_ref, keep_ref, send_ref,
    wt_ref, bcol_ref, rcol_ref, coarse_ref, z1_ref, z2_ref, z3_ref, e_ref, f_ref, acc_ref, bias_ref, outp_ref, line_ref,
    *, groups, grad_scale,
):
    step = pl.program_id(0)
    samples = deriv_ref.shape[0]
    rows = slope_ref.shape[0] // samples
    cells = rows * LANES
    width = x_ref.shape[2]
    my_z, my_x, my_y, my_c = (lax.axis_index(name) for name in ("z", "x", "y", "c"))
    lane = lax.broadcasted_iota(jnp.int32, (1, LANES), 1)

    z_refs = (z1_ref, z2_ref, z3_ref)

    def matmul(s, block):
        z_refs[s - KEPT][...] = nt_dot(wt_ref[...], block)

    @pl.when(step == 0)
    def _():
        wt_ref[...] = (0.5 * w_ref[...].astype(F32)).T.astype(BF16)
        bcol_ref[...] = columns(0.5 * b_ref[...], width)
        rcol_ref[...] = columns(0.5 * r_ref[...].astype(F32).reshape(1, width), width)
        acc_ref[...] = jnp.zeros_like(acc_ref)
        bias_ref[...] = jnp.zeros_like(bias_ref)
        outp_ref[...] = jnp.zeros_like(outp_ref)
        e_ref[...] = jnp.zeros_like(e_ref)
        matmul(1, late_ref[1])
        matmul(2, x_ref[0])
        matmul(3, x_ref[1])
        pairs = same_ref[...] + other_ref[...]
        index = lax.broadcasted_iota(jnp.int32, pairs.shape, 0)
        mine = my_z * 4 + my_x
        slope = jnp.zeros((1, LANES), F32)
        loss = loss_ref[...]
        for group in groups:
            span = group // 2
            base = mine - lax.rem(mine, span)
            inside = jnp.logical_and(index >= base, index < base + span)
            total = jnp.sum(jnp.where(inside, pairs, 0.0), axis=0, keepdims=True)
            more_loss, more_slope = smooth_pair((SHARP / (group * cells)) * total)
            loss = loss + cells * more_loss
            slope = slope + more_slope
        for s in range(samples):
            value = jnp.sum(jnp.where(lane == s, slope, 0.0))
            coarse_ref[s:s + 1, :] = jnp.broadcast_to(value, (1, LANES))
        own = jnp.logical_and(lane >= my_y * samples, lane < (my_y + 1) * samples)
        line_ref[8:9, :] = jnp.where(own, pltpu.roll(loss, my_y * samples, 1), 0.0)
        line_ref[9:16, :] = jnp.zeros((7, LANES), F32)

    quarter = width // 4

    def gradients(s):
        grads = []
        for k in range(CB // LANES):
            row = step * (CB // LANES) + k
            scale = 1.0 + land_ref[pl.ds(row, 1), :].astype(F32)
            local = slope_ref[pl.ds(s * rows + row, 1), :]
            grad = (local + coarse_ref[s:s + 1, :]) * scale
            deriv_ref[s:s + 1, k * LANES:(k + 1) * LANES] = grad
            grads.append(jnp.broadcast_to(grad, (UR, LANES)))
        return grads

    def elementwise(s, out_ref, place, grads, *quarters):
        for u in (u for q in quarters for u in range(q * quarter, (q + 1) * quarter, UR)):
            readout = rcol_ref[u:u + UR, :]
            es = []
            bias = outp = None
            for k in range(CB // LANES):
                span = slice(k * LANES, (k + 1) * LANES)
                if s < KEPT:
                    h = h_ref[s, u:u + UR, span]
                    act = act_ref[s, u:u + UR, span]
                else:
                    z = z_refs[s - KEPT][u:u + UR, span] + bcol_ref[u:u + UR, :]
                    t = jnp.tanh(z)
                    gate = 1.0 + t
                    act = z * gate
                    h = gate + act * (1.0 - t)
                    act = act.astype(BF16)
                e = (readout * grads[k]) * h
                a = act.astype(F32) * grads[k]
                es.append(e.astype(BF16))
                bias = e if bias is None else bias + e
                outp = a if outp is None else outp + a
            out_ref[u:u + UR, place * CB:(place + 1) * CB] = jnp.concatenate(es, axis=1)
            bias_ref[u:u + UR, :] += bias
            outp_ref[u:u + UR, :] += outp

    def accumulate(e, x, half):
        span = slice(half * (width // 2), (half + 1) * (width // 2))
        acc_ref[:, span] += jnp.dot(
            e[...], x[:, :, span].reshape(2 * CB, width // 2), preferred_element_type=F32
        )

    grads = [gradients(s) for s in range(samples)]
    first = functools.partial(elementwise, 2, f_ref, 0, grads[2])
    second = functools.partial(elementwise, 3, f_ref, 1, grads[3])
    third = functools.partial(elementwise, 0, e_ref, 0, grads[0])
    fourth = functools.partial(elementwise, 1, e_ref, 1, grads[1])
    first(0)
    accumulate(e_ref, late_ref, 0)
    first(1, 2)
    accumulate(e_ref, late_ref, 1)
    first(3)
    second(0)
    matmul(2, next_ref[2])
    second(1, 2, 3)
    accumulate(f_ref, x_ref, 0)
    fourth(0, 1)
    matmul(3, next_ref[3])
    fourth(2, 3)
    accumulate(f_ref, x_ref, 1)
    matmul(1, next_ref[1])
    third(0, 1, 2, 3)

    @pl.when(step == pl.num_programs(0) - 1)
    def _():
        accumulate(e_ref, tail_ref, 0)
        accumulate(e_ref, tail_ref, 1)
        acc_ref[...] = (acc_ref[...] * grad_scale).T
        bias = jnp.sum(bias_ref[...].T, axis=0, keepdims=True) * grad_scale
        outp = jnp.sum(outp_ref[...].T, axis=0, keepdims=True) * grad_scale
        for j in range(width // LANES):
            line_ref[j:j + 1, :] = bias[:, j * LANES:(j + 1) * LANES]
            line_ref[4 + j:5 + j, :] = outp[:, j * LANES:(j + 1) * LANES]
        for half, out in ((my_c, keep_ref), (1 - my_c, send_ref)):
            for slot in range(16):
                first = pl.multiple_of(16 * (2 * slot + half), 16)
                for j in range(width // LANES):
                    out[slot * 64 + j * 16:slot * 64 + (j + 1) * 16, :] = acc_ref[
                        pl.ds(first, 16), j * LANES:(j + 1) * LANES
                    ]
            out[1024:1040, :] = line_ref[...]


def in_vmem(array):
    return pltpu.with_memory_space_constraint(array, pltpu.VMEM)


def final_kernel(own_ref, far_ref, inner_ref, offset_ref, loss_ref, *, scale, samples):
    total = own_ref[...] + far_ref[...]
    for j in range(4):
        span = slice(j * LANES, (j + 1) * LANES)
        inner_ref[:, span] = total[j * 16:(j + 1) * 16]
        offset_ref[0:1, span] = total[64 + j:65 + j]
        offset_ref[1:2, span] = total[68 + j:69 + j]
    first = lax.axis_index("y") * samples
    loss_ref[...] = scale * pltpu.roll(total[72:73], lax.rem(LANES - first, LANES), 1)


def whole(shape):
    return pl.BlockSpec(shape, lambda *_: (0,) * len(shape))


def on_device(
    unembed_feature_matrix, weight_in, bias_in, readout_weight, measured_rainfall, land_mask, morton
):
    samples, cells, width = unembed_feature_matrix.shape
    rows = cells // LANES
    tiles = lax.axis_size("z") * lax.axis_size("x") * lax.axis_size("c")
    grad_scale = (width / (samples * lax.axis_size("y") * cells * tiles)) ** 0.5
    steps = cells // CB
    bias_row = bias_in.reshape(1, width)
    readout_row = readout_weight
    land_row = land_mask.reshape(1, cells)
    land_tile = land_mask.reshape(rows, LANES)
    params = pltpu.CompilerParams(
        dimension_semantics=("arbitrary",),
        vmem_limit_bytes=VMEM_LIMIT,
    )
    x_spec = pl.BlockSpec((samples, CF, width), lambda i: (0, i, 0))
    row_spec = pl.BlockSpec((samples, CF), lambda i: (0, i))

    kept_spec = pl.BlockSpec((KEPT, width, CF), lambda i: (i, 0, 0))
    predicted_rainfall, mismatch, totals, bend, activated = pl.pallas_call(
        forward_kernel,
        grid=(cells // CF,),
        in_specs=[
            x_spec, whole((width, width)), whole((1, width)), whole((width,)),
            whole((samples, cells)), whole((1, cells)),
        ],
        out_specs=[
            whole((samples, cells)), whole((samples * rows, LANES)), whole((16, LANES)),
            kept_spec, kept_spec,
        ],
        out_shape=[
            jax.ShapeDtypeStruct((samples, cells), F32),
            jax.ShapeDtypeStruct((samples * rows, LANES), F32),
            jax.ShapeDtypeStruct((16, LANES), F32),
            jax.ShapeDtypeStruct((cells // CF * KEPT, width, CF), F32),
            jax.ShapeDtypeStruct((cells // CF * KEPT, width, CF), BF16),
        ],
        scratch_shapes=[
            pltpu.VMEM((width, width), BF16),
            pltpu.VMEM((width, LANES), F32),
            pltpu.VMEM((16, width), BF16),
        ] + [pltpu.VMEM((width, CF), F32)] * 4 + [pltpu.VMEM((width, CF), BF16)] * 4,
        compiler_params=params,
        name="forward",
    )(
        unembed_feature_matrix, weight_in, bias_row, readout_row, measured_rainfall, land_row,
    )

    kept_spec = pl.BlockSpec((KEPT, width, CB), lambda i: (i // 2, 0, i % 2))
    same_core = lax.all_to_all(totals, ("z", "x"), 0, 0)

    slope, loss = pl.pallas_call(
        tree_kernel,
        out_shape=[
            jax.ShapeDtypeStruct((samples * rows, LANES), F32),
            jax.ShapeDtypeStruct((1, LANES), F32),
        ],
        name="tree",
    )(mismatch, morton.reshape(rows, LANES))

    same_core, slope = lax.optimization_barrier((same_core, slope))
    other_core = lax.ppermute(same_core, "c", [(0, 1), (1, 0)])
    payload = jax.ShapeDtypeStruct((1040, LANES), F32)
    groups = []
    group = 4
    while group < tiles:
        groups.append(group)
        group = group * 4
    groups.append(tiles)
    patch_prediction_deriv, keep, send = pl.pallas_call(
        functools.partial(backward_kernel, groups=tuple(groups), grad_scale=grad_scale),
        grid_spec=pltpu.PrefetchScalarGridSpec(
            num_scalar_prefetch=0,
            grid=(steps,),
            in_specs=[
                pl.BlockSpec((2, CB, width), lambda i: (1, i, 0)),
                pl.BlockSpec((2, CB, width), lambda i: (0, jnp.maximum(i - 1, 0), 0)),
                pl.BlockSpec((4, CB, width), lambda i: (0, jnp.minimum(i + 1, steps - 1), 0)),
                pl.BlockSpec((2, CB, width), lambda i: (0, steps - 1, 0)),
                whole((width, width)), whole((1, width)), whole((width,)),
                whole((samples * rows, LANES)), whole((rows, LANES)),
                pl.BlockSpec(memory_space=pltpu.VMEM), pl.BlockSpec(memory_space=pltpu.VMEM),
                whole((1, LANES)), kept_spec, kept_spec,
            ],
            out_specs=[
                pl.BlockSpec((samples, CB), lambda i: (0, i)),
                whole((1040, LANES)), whole((1040, LANES)),
            ],
            scratch_shapes=[
                pltpu.VMEM((width, width), BF16),
                pltpu.VMEM((width, LANES), F32),
                pltpu.VMEM((width, LANES), F32),
                pltpu.VMEM((8, LANES), F32),
                pltpu.VMEM((width, CB), F32),
                pltpu.VMEM((width, CB), F32),
                pltpu.VMEM((width, CB), F32),
                pltpu.VMEM((width, 2 * CB), BF16),
                pltpu.VMEM((width, 2 * CB), BF16),
                pltpu.VMEM((width, width), F32),
                pltpu.VMEM((width, LANES), F32),
                pltpu.VMEM((width, LANES), F32),
                pltpu.VMEM((16, LANES), F32),
            ],
        ),
        out_shape=[jax.ShapeDtypeStruct((samples, cells), F32), payload, payload],
        compiler_params=params,
        name="backward",
    )(
        *(unembed_feature_matrix,) * 4, weight_in, bias_row, readout_row,
        slope, land_tile, in_vmem(same_core), in_vmem(other_core), loss, bend, activated,
    )

    half = keep + lax.ppermute(send, "c", [(0, 1), (1, 0)])
    line = jnp.broadcast_to(half[1024:][None], (16, 16, LANES))
    slots = jnp.concatenate([half[:1024].reshape(16, 64, LANES), line], axis=1)
    own = jnp.sum(lax.all_to_all(slots, ("z", "x"), 0, 0), axis=0)
    own = own + lax.ppermute(own, "y", [(n, n ^ 1) for n in range(4)])
    far = lax.ppermute(own, "y", [(n, n ^ 3) for n in range(4)])
    inner_coefficient_deriv, offset_projection_derivs, loss_row = pl.pallas_call(
        functools.partial(final_kernel, scale=1.0 / (cells * tiles * SHARP), samples=samples),
        in_specs=[pl.BlockSpec(memory_space=pltpu.VMEM)] * 2,
        out_shape=[
            jax.ShapeDtypeStruct((width // tiles, width), F32),
            jax.ShapeDtypeStruct((2, width), F32),
            jax.ShapeDtypeStruct((1, LANES), F32),
        ],
        compiler_params=pltpu.CompilerParams(vmem_limit_bytes=4 << 20),
        name="final",
    )(in_vmem(own), in_vmem(far))
    penalty_per_example = loss_row[0, :samples]
    return (
        predicted_rainfall,
        patch_prediction_deriv,
        penalty_per_example,
        inner_coefficient_deriv,
        offset_projection_derivs,
    )


def solution(mesh):
    fine = Mesh(mesh.devices.reshape(4, 4, 4, 2), ("y", "z", "x", "c"))
    tile = ("z", "x", "c")
    return jax.shard_map(
        on_device,
        mesh=fine,
        in_specs=(
            P("y", tile, None), P(), P(), P(), P("y", tile), P(tile), P(tile, None),
        ),
        out_specs=(P("y", tile), P("y", tile), P("y"), P(tile, None), P()),
        check_vma=False,
    )
```

```python
import functools

import jax
import jax.numpy as jnp
from jax import lax
from jax.experimental import pallas as pl
from jax.experimental.pallas import tpu as pltpu
from jax.sharding import Mesh, PartitionSpec as P

F32 = jnp.float32
BF16 = jnp.bfloat16
SHARP = 0.5
LANES = 128
CF = 512
CB = 256
UF = 16
UR = 32
VMEM_LIMIT = 56 << 20
KEPT = 1


def nt_dot(a, b):
    return lax.dot_general(a, b, (((1,), (1,)), ((), ())), preferred_element_type=F32)


def columns(row, count):
    return jnp.broadcast_to(row, (LANES, count)).T


def smooth_pair(v):
    root = jnp.sqrt(1.0 + v * v)
    return v * v / (1.0 + root), v / root


def forward_kernel(
    x_ref, w_ref, b_ref, r_ref, meas_ref, land_ref,
    pred_ref, mm_ref, tot_ref, h_ref, act_ref,
    wt_ref, bcol_ref, r8_ref, *rest,
):
    z_refs, spare_refs = rest[:4], rest[4:]
    step = pl.program_id(0)
    samples = x_ref.shape[0]
    rows = mm_ref.shape[0] // samples
    width = w_ref.shape[0]

    @pl.when(step == 0)
    def _():
        wt_ref[...] = (0.5 * w_ref[...].astype(F32)).T.astype(BF16)
        bcol_ref[...] = columns(0.5 * b_ref[...], width)
        r8_ref[...] = jnp.broadcast_to(r_ref[...].astype(F32).reshape(1, width), r8_ref.shape).astype(BF16)

    wt = wt_ref[...]
    readout8 = r8_ref[...]

    def matmul(s):
        z_refs[s][...] = nt_dot(wt, x_ref[s])

    def elementwise(s):
        for u in range(0, width, UF):
            bias = bcol_ref[u:u + UF, :]
            hs, acts = [], []
            for k in range(CF // LANES):
                z = z_refs[s][u:u + UF, k * LANES:(k + 1) * LANES] + bias
                t = jnp.tanh(z)
                gate = 1.0 + t
                act = z * gate
                if s < KEPT:
                    hs.append(gate + act * (1.0 - t))
                acts.append(act.astype(BF16))
            acts = jnp.concatenate(acts, axis=1)
            spare_refs[s][u:u + UF, :] = acts
            if s < KEPT:
                h_ref[s, u:u + UF, :] = jnp.concatenate(hs, axis=1)
                act_ref[s, u:u + UF, :] = acts

    def readout(s, block):
        preds = jnp.dot(readout8, spare_refs[s][...], preferred_element_type=F32)
        for k in range(CF // LANES):
            lane = pl.ds(pl.multiple_of(block * CF + k * LANES, LANES), LANES)
            pred = preds[0:1, k * LANES:(k + 1) * LANES]
            pred_ref[s:s + 1, lane] = pred
            scale = 1.0 + land_ref[:, lane].astype(F32)
            row = s * rows + block * (CF // LANES) + k
            mm_ref[pl.ds(row, 1), :] = scale * (pred - meas_ref[s:s + 1, lane])

    before = jnp.maximum(step - 1, 0)
    readout(0, before)
    readout(1, before)
    elementwise(2)
    matmul(0)
    elementwise(3)
    matmul(1)
    readout(2, before)
    elementwise(0)
    matmul(2)
    readout(3, before)
    elementwise(1)
    matmul(3)

    @pl.when(step == pl.num_programs(0) - 1)
    def _():
        elementwise(2)
        elementwise(3)
        for s in range(samples):
            readout(s, step)
        spot = lax.broadcasted_iota(jnp.int32, tot_ref.shape, 1)
        total = jnp.zeros(tot_ref.shape, F32)
        for s in range(samples):
            value = jnp.sum(mm_ref[s * rows:(s + 1) * rows, :])
            total = total + jnp.where(spot == s, value, 0.0)
        tot_ref[...] = total


def tree_kernel(mm_ref, morton_ref, slope_ref, loss_ref):
    rows = morton_ref.shape[0]
    samples = mm_ref.shape[0] // rows
    total = samples * rows
    cells = rows * LANES
    place = morton_ref[...]
    high = lax.shift_right_logical(place, 7)
    low = jnp.bitwise_and(place, LANES - 1)

    pieces = [jnp.zeros((8, LANES), F32) for _ in range(total // 8)]
    for h in range(rows):
        hits = [high[v:v + 8, :] == h for v in range(0, rows, 8)]
        for s in range(samples):
            source = jnp.broadcast_to(mm_ref[s * rows + h:s * rows + h + 1, :], (8, LANES))
            for v in range(rows // 8):
                moved = jnp.take_along_axis(source, low[v * 8:v * 8 + 8, :], axis=1)
                at = s * (rows // 8) + v
                pieces[at] = jnp.where(hits[v], moved, pieces[at])
    entries = jnp.concatenate(pieces, axis=0)

    lane = lax.broadcasted_iota(jnp.int32, (total, LANES), 1)
    row = lax.broadcasted_iota(jnp.int32, (total, LANES), 0)

    def pair_lane(value, bit):
        other = jnp.where(
            jnp.bitwise_and(lane, bit) == 0,
            pltpu.roll(value, LANES - bit, 1),
            pltpu.roll(value, bit, 1),
        )
        return value + other

    def pair_row(value, bit):
        other = jnp.where(
            jnp.bitwise_and(row, bit) == 0,
            pltpu.roll(value, total - bit, 0),
            pltpu.roll(value, bit, 0),
        )
        return value + other

    loss, slope = smooth_pair(SHARP * entries)
    sums = entries
    node = 1
    while node < cells:
        for bit in (node, 2 * node):
            if bit < LANES:
                sums = pair_lane(sums, bit)
            else:
                sums = pair_row(sums, bit // LANES)
        node = node * 4
        more_loss, more_slope = smooth_pair((SHARP / node) * sums)
        loss = loss + more_loss
        slope = slope + more_slope

    spot = lax.broadcasted_iota(jnp.int32, (1, LANES), 1)
    loss_row = jnp.zeros((1, LANES), F32)
    for s in range(samples):
        value = jnp.sum(loss[s * rows:(s + 1) * rows, :])
        loss_row = loss_row + jnp.where(spot == s, value, 0.0)
    loss_ref[...] = loss_row

    first = slope.astype(BF16).astype(F32)
    rest = slope - first
    second = rest.astype(BF16).astype(F32)
    third = rest - second
    parts = (first, second, third)
    level = lax.broadcasted_iota(jnp.int32, (rows, LANES), 0)
    spread = lax.broadcasted_iota(jnp.int32, (LANES, LANES), 0)
    placed = jnp.zeros((3 * total, LANES), F32)
    for a in range(0, rows, 2):
        left, right = [], []
        for r in (a, a + 1):
            hit = level == high[r:r + 1, :]
            left.append(jnp.concatenate([
                jnp.where(hit, part[s * rows + r:s * rows + r + 1, :], 0.0)
                for part in parts for s in range(samples)
            ], axis=0))
            right.append(jnp.where(spread == low[r:r + 1, :], 1.0, 0.0))
        placed = placed + nt_dot(
            jnp.concatenate(left, axis=1).astype(BF16),
            jnp.concatenate(right, axis=1).astype(BF16),
        )
    slope_ref[...] = placed[:total] + (placed[total:2 * total] + placed[2 * total:])


def backward_kernel(
    x_ref, late_ref, next_ref, tail_ref, w_ref, b_ref, r_ref, slope_ref, land_ref, same_ref, other_ref, loss_ref, h_ref, act_ref,
    deriv_ref, keep_ref, send_ref,
    wt_ref, bcol_ref, rcol_ref, coarse_ref, z1_ref, z2_ref, z3_ref, e_ref, f_ref, acc_ref, bias_ref, outp_ref, line_ref,
    *, groups, grad_scale,
):
    step = pl.program_id(0)
    samples = deriv_ref.shape[0]
    rows = slope_ref.shape[0] // samples
    cells = rows * LANES
    width = x_ref.shape[2]
    my_z, my_x, my_y, my_c = (lax.axis_index(name) for name in ("z", "x", "y", "c"))
    lane = lax.broadcasted_iota(jnp.int32, (1, LANES), 1)

    z_refs = (z1_ref, z2_ref, z3_ref)

    def matmul(s, block):
        z_refs[s - KEPT][...] = nt_dot(wt_ref[...], block)

    @pl.when(step == 0)
    def _():
        wt_ref[...] = (0.5 * w_ref[...].astype(F32)).T.astype(BF16)
        bcol_ref[...] = columns(0.5 * b_ref[...], width)
        rcol_ref[...] = columns(0.5 * r_ref[...].astype(F32).reshape(1, width), width)
        acc_ref[...] = jnp.zeros_like(acc_ref)
        bias_ref[...] = jnp.zeros_like(bias_ref)
        outp_ref[...] = jnp.zeros_like(outp_ref)
        e_ref[...] = jnp.zeros_like(e_ref)
        matmul(1, late_ref[1])
        matmul(2, x_ref[0])
        matmul(3, x_ref[1])
        pairs = same_ref[...] + other_ref[...]
        index = lax.broadcasted_iota(jnp.int32, pairs.shape, 0)
        mine = my_z * 4 + my_x
        slope = jnp.zeros((1, LANES), F32)
        loss = loss_ref[...]
        for group in groups:
            span = group // 2
            base = mine - lax.rem(mine, span)
            inside = jnp.logical_and(index >= base, index < base + span)
            total = jnp.sum(jnp.where(inside, pairs, 0.0), axis=0, keepdims=True)
            more_loss, more_slope = smooth_pair((SHARP / (group * cells)) * total)
            loss = loss + cells * more_loss
            slope = slope + more_slope
        for s in range(samples):
            value = jnp.sum(jnp.where(lane == s, slope, 0.0))
            coarse_ref[s:s + 1, :] = jnp.broadcast_to(value, (1, LANES))
        own = jnp.logical_and(lane >= my_y * samples, lane < (my_y + 1) * samples)
        line_ref[8:9, :] = jnp.where(own, pltpu.roll(loss, my_y * samples, 1), 0.0)
        line_ref[9:16, :] = jnp.zeros((7, LANES), F32)

    quarter = width // 4

    def gradients(s):
        grads = []
        for k in range(CB // LANES):
            row = step * (CB // LANES) + k
            scale = 1.0 + land_ref[pl.ds(row, 1), :].astype(F32)
            local = slope_ref[pl.ds(s * rows + row, 1), :]
            grad = (local + coarse_ref[s:s + 1, :]) * scale
            deriv_ref[s:s + 1, k * LANES:(k + 1) * LANES] = grad
            grads.append(jnp.broadcast_to(grad, (UR, LANES)))
        return grads

    def elementwise(s, out_ref, place, grads, *quarters):
        for u in (u for q in quarters for u in range(q * quarter, (q + 1) * quarter, UR)):
            readout = rcol_ref[u:u + UR, :]
            es = []
            bias = outp = None
            for k in range(CB // LANES):
                span = slice(k * LANES, (k + 1) * LANES)
                if s < KEPT:
                    h = h_ref[s, u:u + UR, span]
                    act = act_ref[s, u:u + UR, span]
                else:
                    z = z_refs[s - KEPT][u:u + UR, span] + bcol_ref[u:u + UR, :]
                    t = jnp.tanh(z)
                    gate = 1.0 + t
                    act = z * gate
                    h = gate + act * (1.0 - t)
                    act = act.astype(BF16)
                e = (readout * grads[k]) * h
                a = act.astype(F32) * grads[k]
                es.append(e.astype(BF16))
                bias = e if bias is None else bias + e
                outp = a if outp is None else outp + a
            out_ref[u:u + UR, place * CB:(place + 1) * CB] = jnp.concatenate(es, axis=1)
            bias_ref[u:u + UR, :] += bias
            outp_ref[u:u + UR, :] += outp

    def accumulate(e, x, half):
        span = slice(half * (width // 2), (half + 1) * (width // 2))
        acc_ref[:, span] += jnp.dot(
            e[...], x[:, :, span].reshape(2 * CB, width // 2), preferred_element_type=F32
        )

    grads = [gradients(s) for s in range(samples)]
    first = functools.partial(elementwise, 2, f_ref, 0, grads[2])
    second = functools.partial(elementwise, 3, f_ref, 1, grads[3])
    third = functools.partial(elementwise, 0, e_ref, 0, grads[0])
    fourth = functools.partial(elementwise, 1, e_ref, 1, grads[1])
    accumulate(e_ref, late_ref, 0)
    first(0, 1, 2, 3)
    matmul(2, next_ref[2])
    accumulate(e_ref, late_ref, 1)
    fourth(0, 1, 2, 3)
    matmul(1, next_ref[1])
    second(0, 1, 2, 3)
    matmul(3, next_ref[3])
    accumulate(f_ref, x_ref, 0)
    accumulate(f_ref, x_ref, 1)
    third(0, 1, 2, 3)

    @pl.when(step == pl.num_programs(0) - 1)
    def _():
        accumulate(e_ref, tail_ref, 0)
        accumulate(e_ref, tail_ref, 1)
        acc_ref[...] = (acc_ref[...] * grad_scale).T
        bias = jnp.sum(bias_ref[...].T, axis=0, keepdims=True) * grad_scale
        outp = jnp.sum(outp_ref[...].T, axis=0, keepdims=True) * grad_scale
        for j in range(width // LANES):
            line_ref[j:j + 1, :] = bias[:, j * LANES:(j + 1) * LANES]
            line_ref[4 + j:5 + j, :] = outp[:, j * LANES:(j + 1) * LANES]
        for half, out in ((my_c, keep_ref), (1 - my_c, send_ref)):
            for slot in range(16):
                first = pl.multiple_of(16 * (2 * slot + half), 16)
                for j in range(width // LANES):
                    out[slot * 64 + j * 16:slot * 64 + (j + 1) * 16, :] = acc_ref[
                        pl.ds(first, 16), j * LANES:(j + 1) * LANES
                    ]
            out[1024:1040, :] = line_ref[...]


def in_vmem(array):
    return pltpu.with_memory_space_constraint(array, pltpu.VMEM)


def final_kernel(own_ref, far_ref, inner_ref, offset_ref, loss_ref, *, scale, samples):
    total = own_ref[...] + far_ref[...]
    for j in range(4):
        span = slice(j * LANES, (j + 1) * LANES)
        inner_ref[:, span] = total[j * 16:(j + 1) * 16]
        offset_ref[0:1, span] = total[64 + j:65 + j]
        offset_ref[1:2, span] = total[68 + j:69 + j]
    first = lax.axis_index("y") * samples
    loss_ref[...] = scale * pltpu.roll(total[72:73], lax.rem(LANES - first, LANES), 1)


def whole(shape):
    return pl.BlockSpec(shape, lambda *_: (0,) * len(shape))


def on_device(
    unembed_feature_matrix, weight_in, bias_in, readout_weight, measured_rainfall, land_mask, morton
):
    samples, cells, width = unembed_feature_matrix.shape
    rows = cells // LANES
    tiles = lax.axis_size("z") * lax.axis_size("x") * lax.axis_size("c")
    grad_scale = (width / (samples * lax.axis_size("y") * cells * tiles)) ** 0.5
    steps = cells // CB
    bias_row = bias_in.reshape(1, width)
    readout_row = readout_weight
    land_row = land_mask.reshape(1, cells)
    land_tile = land_mask.reshape(rows, LANES)
    params = pltpu.CompilerParams(
        dimension_semantics=("arbitrary",),
        vmem_limit_bytes=VMEM_LIMIT,
    )
    x_spec = pl.BlockSpec((samples, CF, width), lambda i: (0, i, 0))
    row_spec = pl.BlockSpec((samples, CF), lambda i: (0, i))

    kept_spec = pl.BlockSpec((KEPT, width, CF), lambda i: (i, 0, 0))
    predicted_rainfall, mismatch, totals, bend, activated = pl.pallas_call(
        forward_kernel,
        grid=(cells // CF,),
        in_specs=[
            x_spec, whole((width, width)), whole((1, width)), whole((width,)),
            whole((samples, cells)), whole((1, cells)),
        ],
        out_specs=[
            whole((samples, cells)), whole((samples * rows, LANES)), whole((16, LANES)),
            kept_spec, kept_spec,
        ],
        out_shape=[
            jax.ShapeDtypeStruct((samples, cells), F32),
            jax.ShapeDtypeStruct((samples * rows, LANES), F32),
            jax.ShapeDtypeStruct((16, LANES), F32),
            jax.ShapeDtypeStruct((cells // CF * KEPT, width, CF), F32),
            jax.ShapeDtypeStruct((cells // CF * KEPT, width, CF), BF16),
        ],
        scratch_shapes=[
            pltpu.VMEM((width, width), BF16),
            pltpu.VMEM((width, LANES), F32),
            pltpu.VMEM((16, width), BF16),
        ] + [pltpu.VMEM((width, CF), F32)] * 4 + [pltpu.VMEM((width, CF), BF16)] * 4,
        compiler_params=params,
        name="forward",
    )(
        unembed_feature_matrix, weight_in, bias_row, readout_row, measured_rainfall, land_row,
    )

    kept_spec = pl.BlockSpec((KEPT, width, CB), lambda i: (i // 2, 0, i % 2))
    same_core = lax.all_to_all(totals, ("z", "x"), 0, 0)

    slope, loss = pl.pallas_call(
        tree_kernel,
        out_shape=[
            jax.ShapeDtypeStruct((samples * rows, LANES), F32),
            jax.ShapeDtypeStruct((1, LANES), F32),
        ],
        compiler_params=pltpu.CompilerParams(

        ),
        name="tree",
    )(mismatch, morton.reshape(rows, LANES))

    same_core, slope = lax.optimization_barrier((same_core, slope))
    other_core = lax.ppermute(same_core, "c", [(0, 1), (1, 0)])
    payload = jax.ShapeDtypeStruct((1040, LANES), F32)
    groups = []
    group = 4
    while group < tiles:
        groups.append(group)
        group = group * 4
    groups.append(tiles)
    patch_prediction_deriv, keep, send = pl.pallas_call(
        functools.partial(backward_kernel, groups=tuple(groups), grad_scale=grad_scale),
        grid_spec=pltpu.PrefetchScalarGridSpec(
            num_scalar_prefetch=0,
            grid=(steps,),
            in_specs=[
                pl.BlockSpec((2, CB, width), lambda i: (1, i, 0)),
                pl.BlockSpec((2, CB, width), lambda i: (0, jnp.maximum(i - 1, 0), 0)),
                pl.BlockSpec((4, CB, width), lambda i: (0, jnp.minimum(i + 1, steps - 1), 0)),
                pl.BlockSpec((2, CB, width), lambda i: (0, steps - 1, 0)),
                whole((width, width)), whole((1, width)), whole((width,)),
                whole((samples * rows, LANES)), whole((rows, LANES)),
                pl.BlockSpec(memory_space=pltpu.VMEM), pl.BlockSpec(memory_space=pltpu.VMEM),
                whole((1, LANES)), kept_spec, kept_spec,
            ],
            out_specs=[
                pl.BlockSpec((samples, CB), lambda i: (0, i)),
                whole((1040, LANES)), whole((1040, LANES)),
            ],
            scratch_shapes=[
                pltpu.VMEM((width, width), BF16),
                pltpu.VMEM((width, LANES), F32),
                pltpu.VMEM((width, LANES), F32),
                pltpu.VMEM((8, LANES), F32),
                pltpu.VMEM((width, CB), F32),
                pltpu.VMEM((width, CB), F32),
                pltpu.VMEM((width, CB), F32),
                pltpu.VMEM((width, 2 * CB), BF16),
                pltpu.VMEM((width, 2 * CB), BF16),
                pltpu.VMEM((width, width), F32),
                pltpu.VMEM((width, LANES), F32),
                pltpu.VMEM((width, LANES), F32),
                pltpu.VMEM((16, LANES), F32),
            ],
        ),
        out_shape=[jax.ShapeDtypeStruct((samples, cells), F32), payload, payload],
        compiler_params=params,
        name="backward",
    )(
        *(unembed_feature_matrix,) * 4, weight_in, bias_row, readout_row,
        slope, land_tile, in_vmem(same_core), in_vmem(other_core), loss, bend, activated,
    )

    half = keep + lax.ppermute(send, "c", [(0, 1), (1, 0)])
    line = jnp.broadcast_to(half[1024:][None], (16, 16, LANES))
    slots = jnp.concatenate([half[:1024].reshape(16, 64, LANES), line], axis=1)
    own = jnp.sum(lax.all_to_all(slots, ("z", "x"), 0, 0), axis=0)
    own = own + lax.ppermute(own, "y", [(n, n ^ 1) for n in range(4)])
    far = lax.ppermute(own, "y", [(n, n ^ 3) for n in range(4)])
    inner_coefficient_deriv, offset_projection_derivs, loss_row = pl.pallas_call(
        functools.partial(final_kernel, scale=1.0 / (cells * tiles * SHARP), samples=samples),
        in_specs=[pl.BlockSpec(memory_space=pltpu.VMEM)] * 2,
        out_shape=[
            jax.ShapeDtypeStruct((width // tiles, width), F32),
            jax.ShapeDtypeStruct((2, width), F32),
            jax.ShapeDtypeStruct((1, LANES), F32),
        ],
        compiler_params=pltpu.CompilerParams(vmem_limit_bytes=4 << 20),
        name="final",
    )(in_vmem(own), in_vmem(far))
    penalty_per_example = loss_row[0, :samples]
    return (
        predicted_rainfall,
        patch_prediction_deriv,
        penalty_per_example,
        inner_coefficient_deriv,
        offset_projection_derivs,
    )


def solution(mesh):
    fine = Mesh(mesh.devices.reshape(4, 4, 4, 2), ("y", "z", "x", "c"))
    tile = ("z", "x", "c")
    return jax.shard_map(
        on_device,
        mesh=fine,
        in_specs=(
            P("y", tile, None), P(), P(), P(), P("y", tile), P(tile), P(tile, None),
        ),
        out_specs=(P("y", tile), P("y", tile), P("y"), P(tile, None), P()),
        check_vma=False,
    )
```
